32 devices in a mesh: groups: 2 (over x), depth: 16 (over z, y, core).
Axes of the slice: x: 2, y: 2, z: 4, core: 2. Of those that a mesh axis runs over, the one named last changes fastest.
Arguments:
- fronts: bfloat16 [4, 64, 8, 2048], P(None, ('groups', 'depth')), parts along dimension 1, may hold values from -6 to 6
- extrap: bfloat16 [32, 16, 5, 2, 128, 128], P('depth'), may hold values from -0.15625 to 0.15625
- offsets: int32 [2, 5], replicated, may hold values from -2 to 2
- assign: int32 [2, 8], replicated, may hold values from 0 to 7, each once within a row
Outputs:
- images: float32 [8, 32, 2048], P(None, ('groups', 'depth')), parts along dimension 1
- last_fronts: bfloat16 [4, 64, 8, 2048], P(None, ('groups', 'depth')), parts along dimension 1
The draws below stay inside these ranges and needn't reach their ends.
There are 2 independent parts, one for each index of `groups`. The reference program is written for one: setup_inputs(seed, part) draws one part's arguments, and reference() takes and returns one part's arrays. A program takes and returns all parts, laid end to end along the dimension named above; an argument that names none is the same for every part. Nothing has to cross between parts.
Inputs may be any that keep to these rules, and one draw needn't show every extreme that they name: `assign`: each row names every shot number once.
All inputs are finite; a program needn't handle non-finite values.
Results may differ from the reference program's by a relative error of at most 0.015.
Values may be sent and summed in bfloat16 or wider, within the bound.
A program may use at most 64 MiB of HBM per device.

```python
import math
import jax
import jax.numpy as jnp
from jax import lax

BLOCK = 128
NBLK = 16
BAND = 5
HANDOVERS = 8
SHOTS = 8
X = 2048
NFREQ = 16
SECTIONS = 2


def plant(result, own_key, smallest, top_value):
    longest = result.shape.index(max(result.shape))
    spots = []
    for shift in (0, 1):
        where = [jax.random.randint(jax.random.fold_in(own_key, axis), (), 0, length) for axis, length in enumerate(result.shape)]
        where[longest] = (where[longest] + shift) % result.shape[longest]
        spots.append(tuple(where))
    return result.at[spots[0]].set(smallest).at[spots[1]].set(top_value)


def block_scale(own_key, extent, split, least, high):
    gain, own = 1.0, jax.random.fold_in(own_key, 6)
    for position, parts in split:
        draws = jnp.exp(jax.random.uniform(jax.random.fold_in(own, position), (parts,), jnp.float32, least / len(split), high / len(split)))
        gain = gain * jnp.repeat(draws, extent[position] // parts).reshape([-1 if axis == position else 1 for axis in range(len(extent))])
    return gain


def noise(own_key, shape, spread, limit, cuts=(), kind=jnp.bfloat16):
    drawn = spread * jax.random.normal(own_key, shape, jnp.float32)
    if cuts:
        drawn = drawn * block_scale(own_key, shape, cuts, -0.22, 0.18)
    return jnp.clip(drawn, -limit, limit).astype(kind)


def setup_inputs(seed: int = 0, part: int = 0) -> dict:
    keys = jax.random.split(jax.random.key(seed), 5)
    part_keys = jax.random.split(jax.random.fold_in(keys[4], part), 5)
    return {
        "fronts": noise(part_keys[0], (4, SECTIONS * NFREQ, SHOTS, X), 1.0, 6.0, ((1, 16),)),
        "extrap": noise(keys[1], (SECTIONS * NFREQ, NBLK, BAND, 2, BLOCK, BLOCK), (2 * BAND * BLOCK) ** -0.5, 0.15625, ((0, 16),)),
        "offsets": plant(jax.random.randint(keys[2], (SECTIONS, BAND), -(BAND // 2), BAND // 2 + 1), jax.random.fold_in(keys[2], 1), -(BAND // 2), (BAND // 2 + 1) - 1).astype(jnp.int32),
        "assign": jax.vmap(lambda own: jax.random.permutation(own, SHOTS))(jax.random.split(keys[3], SECTIONS)).reshape((SECTIONS, SHOTS)).astype(jnp.int32),
    }


def advance(wave_state, band_offsets, operator):
    reach = BAND // 2
    blocks = wave_state.reshape(4, NFREQ, SHOTS, NBLK, BLOCK)
    padded = jnp.pad(blocks, ((0, 0), (0, 0), (0, 0), (reach, reach), (0, 0)))
    shifted = jnp.stack([lax.dynamic_slice_in_dim(padded, band_offsets[band_pos] + reach, NBLK, 3) for band_pos in range(BAND)], axis=3)
    products = jnp.einsum('cfskbj,fbkpjl->pcfsbl', shifted.astype(jnp.float32), operator.astype(jnp.float32), precision=lax.Precision.HIGHEST)
    real_prod = products[0]
    imag_prod = products[1]
    src_real = real_prod[0] - imag_prod[1]
    src_imag = imag_prod[0] + real_prod[1]
    rec_real = real_prod[2] + imag_prod[3]
    rec_imag = real_prod[3] - imag_prod[2]
    joined = jnp.stack([src_real, src_imag, rec_real, rec_imag])
    return joined.reshape(4, NFREQ, SHOTS, X).astype(jnp.bfloat16)

def reference(fronts, extrap, offsets, assign):
    operators = extrap.reshape(SECTIONS, NFREQ, NBLK, BAND, 2, BLOCK, BLOCK)
    wave_state = jnp.moveaxis(fronts.reshape(4, SECTIONS, NFREQ, SHOTS, X), 1, 0)
    image_scale = 1.0 / math.sqrt(2.0 * NFREQ)
    section_rows = jnp.arange(SECTIONS, dtype=jnp.int32)[:, None]
    images = []
    for handover in range(HANDOVERS):
        wave_state = lax.map(lambda section_item: advance(section_item[0], section_item[1], section_item[2]), (wave_state, offsets, operators))
        fields = wave_state.astype(jnp.float32)
        partial_value = image_scale * lax.optimization_barrier(jnp.sum(fields[:, 0] * fields[:, 2] + fields[:, 1] * fields[:, 3], axis=1))
        placed = jnp.zeros_like(partial_value).at[section_rows, assign].set(partial_value)
        images.append(placed.reshape(SECTIONS * SHOTS, X))
        if handover + 1 < HANDOVERS:
            wave_state = jnp.concatenate([wave_state[-1:], wave_state[:-1]], axis=0)
    last_fronts = jnp.moveaxis(wave_state, 0, 1).reshape(4, SECTIONS * NFREQ, SHOTS, X)
    return (jnp.stack(images), last_fronts)
```

```python
import functools
import math

import jax
import jax.numpy as jnp
from jax import lax
from jax.experimental import pallas as pl
from jax.experimental.pallas import tpu as pltpu
from jax.sharding import PartitionSpec as P

HANDOVERS = 8
CHUNKS = 4
MESH = pl.DeviceIdType.MESH


def kernel(
    sections,
    owners,
    offsets_ref,
    assign_ref,
    fronts_ref,
    extrap_ref,
    images_ref,
    last_ref,
    oper,
    padded,
    outbox,
    inbox,
    half_image,
    slot_image,
    image_out,
    image_in,
    load_sem,
    wave_send,
    wave_recv,
    image_send,
    image_recv,
):
    nfield, freqs, slots, _ = fronts_ref.shape
    nblk, band, block = extrap_ref.shape[1], extrap_ref.shape[2], extrap_ref.shape[-1]
    reach = band // 2
    per_chunk = nblk // CHUNKS
    scale = 1.0 / math.sqrt(2.0 * freqs * owners)
    me = lax.axis_index("depth")
    depth = sections * owners
    section = me // owners
    owner = me % owners
    ahead = (me + owners) % depth
    behind = (me + depth - owners) % depth

    def load(freq, chunk):
        rows = pl.ds(chunk * per_chunk, per_chunk)
        return pltpu.make_async_copy(
            extrap_ref.at[freq, rows], oper.at[freq, rows], load_sem.at[freq, chunk]
        )

    for freq in range(freqs):
        for chunk in range(CHUNKS):
            load(freq, chunk).start()

    def mate(step):
        return section * owners + (owner + step) % owners

    barrier = pltpu.get_barrier_semaphore()
    greeted = [ahead] + ([behind] if sections > 2 else []) + [mate(d) for d in range(1, owners)]
    for device in greeted:
        pl.semaphore_signal(barrier, inc=1, device_id={"depth": device}, device_id_type=MESH)

    offs = [offsets_ref[section, k] + reach for k in range(band)]
    slot_of = []
    for shot in range(slots):
        found = jnp.int32(0)
        for slot in range(slots):
            found = jnp.where(assign_ref[section, slot] == shot, slot, found)
        slot_of.append(found)

    blank = jnp.zeros((reach,) + padded.shape[2:], padded.dtype)
    for freq in range(freqs):
        padded[freq, 0:reach] = blank
        padded[freq, reach + nblk : 2 * reach + nblk] = blank
        for b in range(nblk):
            cols = slice(b * block, (b + 1) * block)
            rows = [fronts_ref[c, freq, :, cols].astype(jnp.float32) for c in range(nfield)]
            padded[freq, reach + b] = jnp.concatenate(rows, axis=0).astype(padded.dtype)

    def wave_copy(rnd, freq, rows):
        return pltpu.make_async_remote_copy(
            src_ref=outbox.at[rnd, freq, rows],
            dst_ref=inbox.at[rnd, freq, rows],
            send_sem=wave_send.at[rnd, freq],
            recv_sem=wave_recv.at[rnd, freq],
            device_id={"depth": ahead},
            device_id_type=MESH,
        )

    def image_copy(rnd, step):
        return pltpu.make_async_remote_copy(
            src_ref=image_out.at[rnd, step],
            dst_ref=image_in.at[rnd, step],
            send_sem=image_send.at[rnd],
            recv_sem=image_recv.at[rnd],
            device_id={"depth": mate(step)},
            device_id_type=MESH,
        )

    def image_all(rnd):
        return pltpu.make_async_remote_copy(
            src_ref=image_out.at[rnd, pl.ds(1, owners - 1)],
            dst_ref=image_in.at[rnd, pl.ds(1, owners - 1)],
            send_sem=image_send.at[rnd],
            recv_sem=image_recv.at[rnd],
            device_id={"depth": ahead},
            device_id_type=MESH,
        )

    def one_block(rnd, freq, b, last):
        lhs = jnp.concatenate([padded[freq, b + offs[k]] for k in range(band)], axis=1)
        rhs = jnp.concatenate(
            [
                jnp.concatenate([oper[freq, b, k, 0], oper[freq, b, k, 1]], axis=1)
                for k in range(band)
            ],
            axis=0,
        )
        both = jnp.dot(lhs, rhs, preferred_element_type=jnp.float32)
        re = [both[c * slots : (c + 1) * slots, :block] for c in range(nfield)]
        im = [both[c * slots : (c + 1) * slots, block:] for c in range(nfield)]
        new = [re[0] - im[1], im[0] + re[1], re[2] + im[3], re[3] - im[2]]
        rounded = jnp.concatenate(new, axis=0).astype(jnp.bfloat16)
        if last:
            cols = pl.ds(pl.multiple_of(b * block, block), block)
            for c in range(nfield):
                last_ref[c, freq, :, cols] = new[c].astype(jnp.bfloat16)
        else:
            outbox[rnd, freq, b] = rounded
        wide = rounded.astype(jnp.float32)
        part = [wide[c * slots : (c + 1) * slots] for c in range(nfield)]
        image = part[0] * part[2] + part[1] * part[3]
        if freq > 0:
            image = image + half_image[b]
        if freq < freqs - 1:
            half_image[b] = image
        else:
            for slot in range(slots):
                slot_image[slot, pl.ds(b, 1), :] = image[slot : slot + 1] * scale

    def advance(rnd, first=False, last=False):
        for freq in range(freqs):
            if not first:
                wave_copy(rnd - 1, freq, pl.ds(0, nblk)).wait_recv()
                padded[freq, reach : reach + nblk] = inbox[rnd - 1, freq]

            def chunk_body(chunk):
                if first:
                    load(freq, chunk).wait()
                for i in range(per_chunk):
                    one_block(rnd, freq, chunk * per_chunk + i, last)
                if first and freq == 0 and chunk == 0:
                    pl.semaphore_wait(barrier, len(greeted))
                if not last:
                    wave_copy(rnd, freq, pl.ds(chunk * per_chunk, per_chunk)).start()

            if first:
                for chunk in range(CHUNKS):
                    chunk_body(chunk)
            else:
                pl.loop(0, CHUNKS)(chunk_body)
        for step in range(owners):
            target = (owner + step) % owners
            chosen = slot_of[0]
            for shot in range(1, slots):
                chosen = jnp.where(target == shot, slot_of[shot], chosen)
            image_out[rnd, step] = slot_image[chosen]
        for step in range(1, owners):
            image_copy(rnd, step).start()

    def finish_image(rnd):
        image_all(rnd).wait_recv()
        total = image_out[rnd, 0]
        for step in range(1, owners):
            total = total + image_in[rnd, step]
        images_ref[rnd] = total

    advance(0, first=True)

    @pl.loop(1, HANDOVERS - 1)
    def _(rnd):
        advance(rnd)
        finish_image(rnd - 1)

    advance(HANDOVERS - 1, last=True)
    finish_image(HANDOVERS - 2)

    @pl.loop(0, HANDOVERS - 1)
    def _(rnd):
        for freq in range(freqs):
            wave_copy(rnd, freq, pl.ds(0, nblk)).wait_send()
        image_all(rnd).wait_send()

    finish_image(HANDOVERS - 1)
    image_all(HANDOVERS - 1).wait_send()


def on_device(sections, owners, fronts, extrap, offsets, assign):
    nfield, freqs, slots, points = fronts.shape
    _, nblk, band, _, block, _ = extrap.shape
    moves = HANDOVERS - 1
    wave = (moves, freqs, nblk, nfield * slots, block)
    image = (HANDOVERS, owners, nblk, block)
    vmem = pl.BlockSpec(memory_space=pltpu.VMEM)
    smem = pl.BlockSpec(memory_space=pltpu.SMEM)
    images, last = pl.pallas_call(
        functools.partial(kernel, sections, owners),
        out_shape=(
            jax.ShapeDtypeStruct((HANDOVERS, nblk, block), jnp.float32),
            jax.ShapeDtypeStruct(fronts.shape, fronts.dtype),
        ),
        in_specs=[smem, smem, vmem, pl.BlockSpec(memory_space=pl.ANY)],
        out_specs=(vmem, vmem),
        scratch_shapes=[
            pltpu.VMEM(extrap.shape, extrap.dtype),
            pltpu.VMEM((freqs, nblk + 2 * (band // 2), nfield * slots, block), fronts.dtype),
            pltpu.VMEM(wave, fronts.dtype),
            pltpu.VMEM(wave, fronts.dtype),
            pltpu.VMEM((nblk, slots, block), jnp.float32),
            pltpu.VMEM((slots, nblk, block), jnp.float32),
            pltpu.VMEM(image, jnp.float32),
            pltpu.VMEM(image, jnp.float32),
            pltpu.SemaphoreType.DMA((freqs, CHUNKS)),
            pltpu.SemaphoreType.DMA((moves, freqs)),
            pltpu.SemaphoreType.DMA((moves, freqs)),
            pltpu.SemaphoreType.DMA((HANDOVERS,)),
            pltpu.SemaphoreType.DMA((HANDOVERS,)),
        ],
        compiler_params=pltpu.CompilerParams(collective_id=0, has_side_effects=True),
    )(offsets, assign, fronts, extrap)
    return images.reshape(HANDOVERS, slots // owners, points), last


def solution(mesh):
    depth = mesh.shape["depth"]

    def program(fronts, extrap, offsets, assign):
        sections = offsets.shape[0]
        placed = (
            P(None, ("groups", "depth"), None, None),
            P("depth", None, None, None, None, None),
            P(),
            P(),
        )
        return jax.shard_map(
            functools.partial(on_device, sections, depth // sections),
            mesh=mesh,
            in_specs=placed,
            out_specs=(
                P(None, ("groups", "depth"), None),
                P(None, ("groups", "depth"), None, None),
            ),
            check_vma=False,
        )(fronts, extrap, offsets, assign)

    return program
```

```python
import functools
import math

import jax
import jax.numpy as jnp
from jax import lax
from jax.experimental import pallas as pl
from jax.experimental.pallas import tpu as pltpu
from jax.sharding import PartitionSpec as P

HANDOVERS = 8
PARTS = 4
VMEM_BYTES = 48 << 20
MESH = pl.DeviceIdType.MESH


def cuts(total, ends):
    edges = [0] + [e for e in ends if 0 < e < total] + [total]
    return list(zip(edges[:-1], edges[1:]))


def kernel(
    sections,
    owners,
    offsets_ref,
    assign_ref,
    fronts_hbm,
    extrap_ref,
    images_ref,
    last_ref,
    fronts_ref,
    oper,
    padded,
    outbox,
    inbox,
    half_image,
    slot_image,
    near_out,
    near_in,
    mate_out,
    mate_in,
    tail_out,
    tail_in,
    front_sem,
    load_sem,
    wave_send,
    wave_recv,
    near_send,
    near_recv,
    mate_send,
    mate_recv,
    tail_send,
    tail_recv,
):
    nfield, freqs, slots, _ = fronts_ref.shape
    nblk, band, block = extrap_ref.shape[1], extrap_ref.shape[2], extrap_ref.shape[-1]
    reach = band // 2
    half = owners // 2
    scale = 1.0 / math.sqrt(2.0 * freqs * owners)
    final = HANDOVERS - 1
    me = lax.axis_index("depth")
    depth = sections * owners
    section = me // owners
    owner = me % owners
    upper = owner // half
    lane = owner % half
    ahead = (me + owners) % depth
    behind = (me + depth - owners) % depth

    groups = cuts(nblk, (6, 12))
    parts = cuts(nblk, (6, 14))
    halves = cuts(nblk, (nblk // 2,))

    def front_load(freq):
        return pltpu.make_async_copy(
            fronts_hbm.at[:, freq], fronts_ref.at[:, freq], front_sem.at[freq]
        )

    def load(freq, part):
        lo, hi = groups[part]
        rows = pl.ds(lo, hi - lo)
        return pltpu.make_async_copy(
            extrap_ref.at[freq, rows], oper.at[freq, rows], load_sem.at[freq, part]
        )

    for freq in range(freqs):
        front_load(freq).start()
        for part in range(len(groups)):
            load(freq, part).start()

    def near(step):
        return section * owners + upper * half + (lane + step) % half

    def any_mate(step):
        return section * owners + (owner + step) % owners

    mate = section * owners + (owner + half) % owners
    barrier = pltpu.get_barrier_semaphore()
    greeted = [ahead] + ([behind] if sections > 2 else [])
    greeted = greeted + [any_mate(d) for d in range(1, owners)]
    for device in greeted:
        pl.semaphore_signal(barrier, inc=1, device_id={"depth": device}, device_id_type=MESH)

    offs = [offsets_ref[section, k] + reach for k in range(band)]
    slot_of = []
    for shot in range(slots):
        found = jnp.int32(0)
        for slot in range(slots):
            found = jnp.where(assign_ref[section, slot] == shot, slot, found)
        slot_of.append(found)

    def slot_for(target):
        chosen = slot_of[0]
        for shot in range(1, slots):
            chosen = jnp.where(target == shot, slot_of[shot], chosen)
        return chosen

    blank = jnp.zeros((reach,) + padded.shape[2:], padded.dtype)
    for freq in range(freqs):
        padded[freq, 0:reach] = blank
        padded[freq, reach + nblk : 2 * reach + nblk] = blank

    def unpack_front(freq):
        front_load(freq).wait()
        for b in range(nblk):
            cols = slice(b * block, (b + 1) * block)
            rows = [fronts_ref[c, freq, :, cols].astype(jnp.float32) for c in range(nfield)]
            padded[freq, reach + b] = jnp.concatenate(rows, axis=0).astype(padded.dtype)

    def remote(src, dst, send, recv, device):
        return pltpu.make_async_remote_copy(
            src_ref=src,
            dst_ref=dst,
            send_sem=send,
            recv_sem=recv,
            device_id={"depth": device},
            device_id_type=MESH,
        )

    def wave_copy(rnd, freq, part, lo, size):
        rows = pl.ds(lo, size)
        return remote(
            outbox.at[rnd, freq, rows],
            inbox.at[rnd, freq, rows],
            wave_send.at[rnd, freq, part],
            wave_recv.at[rnd, freq, part],
            ahead,
        )

    def near_copy(rnd, lo, size, device):
        rows = pl.ds(lo, size)
        return remote(
            near_out.at[rnd, rows],
            near_in.at[rnd, rows],
            near_send.at[rnd],
            near_recv.at[rnd],
            device,
        )

    def mate_copy(rnd):
        return remote(
            mate_out.at[rnd], mate_in.at[rnd], mate_send.at[rnd], mate_recv.at[rnd], mate
        )

    def tail_copy(piece, lo, size, device):
        rows = pl.ds(lo, size)
        return remote(
            tail_out.at[piece, rows],
            tail_in.at[piece, rows],
            tail_send.at[piece],
            tail_recv.at[piece],
            device,
        )

    def one_block(rnd, freq, b):
        lhs = jnp.concatenate([padded[freq, b + offs[k]] for k in range(band)], axis=1)
        rhs = jnp.concatenate(
            [
                jnp.concatenate([oper[freq, b, k, 0], oper[freq, b, k, 1]], axis=1)
                for k in range(band)
            ],
            axis=0,
        )
        both = jnp.dot(lhs, rhs, preferred_element_type=jnp.float32)
        re = [both[c * slots : (c + 1) * slots, :block] for c in range(nfield)]
        im = [both[c * slots : (c + 1) * slots, block:] for c in range(nfield)]
        new = [re[0] - im[1], im[0] + re[1], re[2] + im[3], re[3] - im[2]]
        rounded = jnp.concatenate(new, axis=0).astype(jnp.bfloat16)
        outbox[rnd, freq, b] = rounded
        wide = rounded.astype(jnp.float32)
        part = [wide[c * slots : (c + 1) * slots] for c in range(nfield)]
        image = part[0] * part[2] + part[1] * part[3]
        if freq > 0:
            image = image + half_image[b]
        if freq < freqs - 1:
            half_image[b] = image
        else:
            for slot in range(slots):
                slot_image[slot, pl.ds(b, 1), :] = image[slot : slot + 1] * scale

    def send_near(rnd):
        for step in range(half):
            column = (lane + step) % half
            near_out[rnd, step, 0] = slot_image[slot_for(upper * half + column)]
            near_out[rnd, step, 1] = slot_image[slot_for((1 - upper) * half + column)]
        for step in range(1, half):
            near_copy(rnd, step, 1, near(step)).start()

    def send_mate(rnd):
        near_copy(rnd, 1, half - 1, mate).wait_recv()
        mine = near_out[rnd, 0, 0]
        other = near_out[rnd, 0, 1]
        for step in range(1, half):
            mine = mine + near_in[rnd, step, 0]
            other = other + near_in[rnd, step, 1]
        images_ref[rnd] = mine
        mate_out[rnd] = other
        mate_copy(rnd).start()

    def finish_image(rnd):
        mate_copy(rnd).wait_recv()
        images_ref[rnd] = images_ref[rnd] + mate_in[rnd]

    def send_tail(piece):
        lo, hi = halves[piece]
        for step in range(owners):
            tail_out[piece, step] = slot_image[slot_for((owner + step) % owners), lo:hi]
        for step in range(1, owners):
            tail_copy(piece, step, 1, any_mate(step)).start()

    @pl.loop(0, HANDOVERS)
    def _(rnd):
        for freq in range(freqs):
            closing = freq == freqs - 1
            have = 0
            sent = 0
            imaged = 0
            for group, (lo, hi) in enumerate(groups):
                need = min(hi + reach, nblk)
                fresh = []
                while have < len(parts) and (parts[have][0] < need):
                    fresh.append(have)
                    have += 1

                @pl.when(rnd == 0)
                def _():
                    if group == 0:
                        unpack_front(freq)
                    load(freq, group).wait()

                @pl.when(rnd > 0)
                def _():
                    for part in fresh:
                        start, end = parts[part]
                        wave_copy(rnd - 1, freq, part, start, end - start).wait_recv()
                        padded[freq, reach + start : reach + end] = inbox[
                            rnd - 1, freq, start:end
                        ]

                for b in range(lo, hi):
                    one_block(rnd, freq, b)

                if freq == 0 and group == 0:

                    @pl.when(rnd == 0)
                    def _():
                        pl.semaphore_wait(barrier, len(greeted))

                outgoing = []
                while sent < len(parts) and parts[sent][1] <= hi:
                    outgoing.append(sent)
                    sent += 1

                @pl.when(rnd < final)
                def _():
                    for part in outgoing:
                        start, end = parts[part]
                        wave_copy(rnd, freq, part, start, end - start).start()

                @pl.when(rnd == final)
                def _():
                    nonlocal imaged
                    while closing and imaged < len(halves) and halves[imaged][1] <= hi:
                        send_tail(imaged)
                        imaged += 1
                    for b in range(lo, hi):
                        cols = slice(b * block, (b + 1) * block)
                        for c in range(nfield):
                            rows = slice(c * slots, (c + 1) * slots)
                            last_ref[c, freq, :, cols] = outbox[rnd, freq, b, rows, :]

            if freq == freqs - 2:

                @pl.when(rnd > 0)
                def _():
                    send_mate(rnd - 1)

        @pl.when(rnd < final)
        def _():
            send_near(rnd)

        @pl.when((rnd > 1) & (rnd < final))
        def _():
            finish_image(rnd - 2)

    @pl.loop(0, final)
    def _(rnd):
        for freq in range(freqs):
            for part, (lo, hi) in enumerate(parts):
                wave_copy(rnd, freq, part, lo, hi - lo).wait_send()
        near_copy(rnd, 1, half - 1, mate).wait_send()
        mate_copy(rnd).wait_send()

    finish_image(final - 2)
    finish_image(final - 1)
    for piece, (lo, hi) in enumerate(halves):
        tail_copy(piece, 1, owners - 1, mate).wait_recv()
        total = tail_out[piece, 0]
        for step in range(1, owners):
            total = total + tail_in[piece, step]
        images_ref[final, lo:hi] = total
    for piece in range(len(halves)):
        tail_copy(piece, 1, owners - 1, mate).wait_send()


def on_device(sections, owners, fronts, extrap, offsets, assign):
    nfield, freqs, slots, points = fronts.shape
    _, nblk, band, _, block, _ = extrap.shape
    moves = HANDOVERS - 1
    wave = (moves, freqs, nblk, nfield * slots, block)
    near = (moves, owners // 2, 2, nblk, block)
    mate = (moves, nblk, block)
    tail = (2, owners, nblk // 2, block)
    vmem = pl.BlockSpec(memory_space=pltpu.VMEM)
    smem = pl.BlockSpec(memory_space=pltpu.SMEM)
    hbm = pl.BlockSpec(memory_space=pltpu.HBM)
    dma = pltpu.SemaphoreType.DMA
    images, last = pl.pallas_call(
        functools.partial(kernel, sections, owners),
        out_shape=(
            jax.ShapeDtypeStruct((HANDOVERS, nblk, block), jnp.float32),
            jax.ShapeDtypeStruct(fronts.shape, fronts.dtype),
        ),
        in_specs=[smem, smem, hbm, hbm],
        out_specs=(vmem, vmem),
        scratch_shapes=[
            pltpu.VMEM(fronts.shape, fronts.dtype),
            pltpu.VMEM(extrap.shape, extrap.dtype),
            pltpu.VMEM((freqs, nblk + 2 * (band // 2), nfield * slots, block), fronts.dtype),
            pltpu.VMEM((HANDOVERS,) + wave[1:], fronts.dtype),
            pltpu.VMEM(wave, fronts.dtype),
            pltpu.VMEM((nblk, slots, block), jnp.float32),
            pltpu.VMEM((slots, nblk, block), jnp.float32),
            pltpu.VMEM(near, jnp.float32),
            pltpu.VMEM(near, jnp.float32),
            pltpu.VMEM(mate, jnp.float32),
            pltpu.VMEM(mate, jnp.float32),
            pltpu.VMEM(tail, jnp.float32),
            pltpu.VMEM(tail, jnp.float32),
            dma((freqs,)),
            dma((freqs, PARTS)),
            dma((moves, freqs, PARTS)),
            dma((moves, freqs, PARTS)),
            dma((moves,)),
            dma((moves,)),
            dma((moves,)),
            dma((moves,)),
            dma((2,)),
            dma((2,)),
        ],
        compiler_params=pltpu.CompilerParams(
            collective_id=0, has_side_effects=True, vmem_limit_bytes=VMEM_BYTES
        ),
    )(offsets, assign, fronts, extrap)
    return images.reshape(HANDOVERS, slots // owners, points), last


def solution(mesh):
    depth = mesh.shape["depth"]

    def program(fronts, extrap, offsets, assign):
        sections = offsets.shape[0]
        placed = (
            P(None, ("groups", "depth"), None, None),
            P("depth", None, None, None, None, None),
            P(),
            P(),
        )
        return jax.shard_map(
            functools.partial(on_device, sections, depth // sections),
            mesh=mesh,
            in_specs=placed,
            out_specs=(
                P(None, ("groups", "depth"), None),
                P(None, ("groups", "depth"), None, None),
            ),
            check_vma=False,
        )(fronts, extrap, offsets, assign)

    return program
```

```python
import functools
import math

import jax
import jax.numpy as jnp
from jax import lax
from jax.experimental import pallas as pl
from jax.experimental.pallas import tpu as pltpu
from jax.sharding import PartitionSpec as P

HANDOVERS = 8
PARTS = 4
VMEM_BYTES = 48 << 20
MESH = pl.DeviceIdType.MESH


def cuts(total, ends):
    edges = [0] + [e for e in ends if 0 < e < total] + [total]
    return list(zip(edges[:-1], edges[1:]))


def kernel(
    sections,
    owners,
    offsets_ref,
    assign_ref,
    fronts_hbm,
    extrap_ref,
    images_ref,
    last_ref,
    fronts_ref,
    oper,
    padded,
    outbox,
    inbox,
    half_image,
    slot_image,
    near_out,
    near_in,
    mate_out,
    mate_in,
    tail_out,
    tail_in,
    front_sem,
    load_sem,
    wave_send,
    wave_recv,
    near_send,
    near_recv,
    mate_send,
    mate_recv,
    tail_send,
    tail_recv,
):
    nfield, freqs, slots, _ = fronts_ref.shape
    nblk, band, block = extrap_ref.shape[1], extrap_ref.shape[2], extrap_ref.shape[-1]
    reach = band // 2
    half = owners // 2
    scale = 1.0 / math.sqrt(2.0 * freqs * owners)
    final = HANDOVERS - 1
    me = lax.axis_index("depth")
    depth = sections * owners
    section = me // owners
    owner = me % owners
    upper = owner // half
    lane = owner % half
    ahead = (me + owners) % depth
    behind = (me + depth - owners) % depth

    groups = cuts(nblk, (2, 8, 12))
    parts = cuts(nblk, (2, 8, 14))
    halves = cuts(nblk, (nblk // 2,))

    def front_load(freq):
        return pltpu.make_async_copy(
            fronts_hbm.at[:, freq], fronts_ref.at[:, freq], front_sem.at[freq]
        )

    def load(freq, part):
        lo, hi = groups[part]
        rows = pl.ds(lo, hi - lo)
        return pltpu.make_async_copy(
            extrap_ref.at[freq, rows], oper.at[freq, rows], load_sem.at[freq, part]
        )

    for freq in range(freqs):
        front_load(freq).start()
        for part in range(len(groups)):
            load(freq, part).start()

    def near(step):
        return section * owners + upper * half + (lane + step) % half

    def any_mate(step):
        return section * owners + (owner + step) % owners

    mate = section * owners + (owner + half) % owners
    barrier = pltpu.get_barrier_semaphore()
    greeted = [ahead] + ([behind] if sections > 2 else [])
    greeted = greeted + [any_mate(d) for d in range(1, owners)]
    for device in greeted:
        pl.semaphore_signal(barrier, inc=1, device_id={"depth": device}, device_id_type=MESH)

    offs = [offsets_ref[section, k] + reach for k in range(band)]
    slot_of = []
    for shot in range(slots):
        found = jnp.int32(0)
        for slot in range(slots):
            found = jnp.where(assign_ref[section, slot] == shot, slot, found)
        slot_of.append(found)

    def slot_for(target):
        chosen = slot_of[0]
        for shot in range(1, slots):
            chosen = jnp.where(target == shot, slot_of[shot], chosen)
        return chosen

    blank = jnp.zeros((reach,) + padded.shape[2:], padded.dtype)
    for freq in range(freqs):
        padded[freq, 0:reach] = blank
        padded[freq, reach + nblk : 2 * reach + nblk] = blank

    def unpack_front(freq):
        front_load(freq).wait()
        for b in range(nblk):
            cols = slice(b * block, (b + 1) * block)
            rows = [fronts_ref[c, freq, :, cols].astype(jnp.float32) for c in range(nfield)]
            padded[freq, reach + b] = jnp.concatenate(rows, axis=0).astype(padded.dtype)

    def remote(src, dst, send, recv, device):
        return pltpu.make_async_remote_copy(
            src_ref=src,
            dst_ref=dst,
            send_sem=send,
            recv_sem=recv,
            device_id={"depth": device},
            device_id_type=MESH,
        )

    def wave_copy(rnd, freq, part, lo, size):
        rows = pl.ds(lo, size)
        return remote(
            outbox.at[rnd, freq, rows],
            inbox.at[rnd, freq, rows],
            wave_send.at[rnd, freq, part],
            wave_recv.at[rnd, freq, part],
            ahead,
        )

    def near_copy(rnd, lo, size, device):
        rows = pl.ds(lo, size)
        return remote(
            near_out.at[rnd, rows],
            near_in.at[rnd, rows],
            near_send.at[rnd],
            near_recv.at[rnd],
            device,
        )

    def mate_copy(rnd):
        return remote(
            mate_out.at[rnd], mate_in.at[rnd], mate_send.at[rnd], mate_recv.at[rnd], mate
        )

    def tail_copy(piece, lo, size, device):
        rows = pl.ds(lo, size)
        return remote(
            tail_out.at[piece, rows],
            tail_in.at[piece, rows],
            tail_send.at[piece],
            tail_recv.at[piece],
            device,
        )

    def one_block(rnd, freq, b):
        lhs = jnp.concatenate([padded[freq, b + offs[k]] for k in range(band)], axis=1)
        rhs = jnp.concatenate(
            [
                jnp.concatenate([oper[freq, b, k, 0], oper[freq, b, k, 1]], axis=1)
                for k in range(band)
            ],
            axis=0,
        )
        both = jnp.dot(lhs, rhs, preferred_element_type=jnp.float32)
        re = [both[c * slots : (c + 1) * slots, :block] for c in range(nfield)]
        im = [both[c * slots : (c + 1) * slots, block:] for c in range(nfield)]
        new = [re[0] - im[1], im[0] + re[1], re[2] + im[3], re[3] - im[2]]
        rounded = jnp.concatenate(new, axis=0).astype(jnp.bfloat16)
        outbox[rnd, freq, b] = rounded
        wide = rounded.astype(jnp.float32)
        part = [wide[c * slots : (c + 1) * slots] for c in range(nfield)]
        image = part[0] * part[2] + part[1] * part[3]
        if freq > 0:
            image = image + half_image[b]
        if freq < freqs - 1:
            half_image[b] = image
        else:
            for slot in range(slots):
                slot_image[slot, pl.ds(b, 1), :] = image[slot : slot + 1] * scale

    def send_near(rnd):
        for step in range(half):
            column = (lane + step) % half
            near_out[rnd, step, 0] = slot_image[slot_for(upper * half + column)]
            near_out[rnd, step, 1] = slot_image[slot_for((1 - upper) * half + column)]
        for step in range(1, half):
            near_copy(rnd, step, 1, near(step)).start()

    def send_mate(rnd):
        near_copy(rnd, 1, half - 1, mate).wait_recv()
        mine = near_out[rnd, 0, 0]
        other = near_out[rnd, 0, 1]
        for step in range(1, half):
            mine = mine + near_in[rnd, step, 0]
            other = other + near_in[rnd, step, 1]
        images_ref[rnd] = mine
        mate_out[rnd] = other
        mate_copy(rnd).start()

    def finish_image(rnd):
        mate_copy(rnd).wait_recv()
        images_ref[rnd] = images_ref[rnd] + mate_in[rnd]

    def send_tail(piece):
        lo, hi = halves[piece]
        for step in range(owners):
            tail_out[piece, step] = slot_image[slot_for((owner + step) % owners), lo:hi]
        for step in range(1, owners):
            tail_copy(piece, step, 1, any_mate(step)).start()

    @pl.loop(0, HANDOVERS)
    def _(rnd):
        for freq in range(freqs):
            closing = freq == freqs - 1
            have = 0
            sent = 0
            imaged = 0
            for group, (lo, hi) in enumerate(groups):
                need = min(hi + reach, nblk)
                fresh = []
                while have < len(parts) and (parts[have][0] < need):
                    fresh.append(have)
                    have += 1

                @pl.when(rnd == 0)
                def _():
                    if group == 0:
                        unpack_front(freq)
                    load(freq, group).wait()

                @pl.when(rnd > 0)
                def _():
                    for part in fresh:
                        start, end = parts[part]
                        wave_copy(rnd - 1, freq, part, start, end - start).wait_recv()
                        padded[freq, reach + start : reach + end] = inbox[
                            rnd - 1, freq, start:end
                        ]

                for b in range(lo, hi):
                    one_block(rnd, freq, b)

                if freq == 0 and group == 0:

                    @pl.when(rnd == 0)
                    def _():
                        pl.semaphore_wait(barrier, len(greeted))

                outgoing = []
                while sent < len(parts) and parts[sent][1] <= hi:
                    outgoing.append(sent)
                    sent += 1

                @pl.when(rnd < final)
                def _():
                    for part in outgoing:
                        start, end = parts[part]
                        wave_copy(rnd, freq, part, start, end - start).start()

                @pl.when(rnd == final)
                def _():
                    nonlocal imaged
                    while closing and imaged < len(halves) and halves[imaged][1] <= hi:
                        send_tail(imaged)
                        imaged += 1
                    for b in range(lo, hi):
                        cols = slice(b * block, (b + 1) * block)
                        for c in range(nfield):
                            rows = slice(c * slots, (c + 1) * slots)
                            last_ref[c, freq, :, cols] = outbox[rnd, freq, b, rows, :]

            if freq == freqs - 2:

                @pl.when(rnd > 0)
                def _():
                    send_mate(rnd - 1)

        @pl.when(rnd < final)
        def _():
            send_near(rnd)

        @pl.when((rnd > 1) & (rnd < final))
        def _():
            finish_image(rnd - 2)

    @pl.loop(0, final)
    def _(rnd):
        for freq in range(freqs):
            for part, (lo, hi) in enumerate(parts):
                wave_copy(rnd, freq, part, lo, hi - lo).wait_send()
        near_copy(rnd, 1, half - 1, mate).wait_send()
        mate_copy(rnd).wait_send()

    finish_image(final - 2)
    finish_image(final - 1)
    for piece, (lo, hi) in enumerate(halves):
        tail_copy(piece, 1, owners - 1, mate).wait_recv()
        total = tail_out[piece, 0]
        for step in range(1, owners):
            total = total + tail_in[piece, step]
        images_ref[final, lo:hi] = total
    for piece in range(len(halves)):
        tail_copy(piece, 1, owners - 1, mate).wait_send()


def on_device(sections, owners, fronts, extrap, offsets, assign):
    nfield, freqs, slots, points = fronts.shape
    _, nblk, band, _, block, _ = extrap.shape
    moves = HANDOVERS - 1
    wave = (moves, freqs, nblk, nfield * slots, block)
    near = (moves, owners // 2, 2, nblk, block)
    mate = (moves, nblk, block)
    tail = (2, owners, nblk // 2, block)
    vmem = pl.BlockSpec(memory_space=pltpu.VMEM)
    smem = pl.BlockSpec(memory_space=pltpu.SMEM)
    hbm = pl.BlockSpec(memory_space=pltpu.HBM)
    dma = pltpu.SemaphoreType.DMA
    images, last = pl.pallas_call(
        functools.partial(kernel, sections, owners),
        out_shape=(
            jax.ShapeDtypeStruct((HANDOVERS, nblk, block), jnp.float32),
            jax.ShapeDtypeStruct(fronts.shape, fronts.dtype),
        ),
        in_specs=[smem, smem, hbm, hbm],
        out_specs=(vmem, vmem),
        scratch_shapes=[
            pltpu.VMEM(fronts.shape, fronts.dtype),
            pltpu.VMEM(extrap.shape, extrap.dtype),
            pltpu.VMEM((freqs, nblk + 2 * (band // 2), nfield * slots, block), fronts.dtype),
            pltpu.VMEM((HANDOVERS,) + wave[1:], fronts.dtype),
            pltpu.VMEM(wave, fronts.dtype),
            pltpu.VMEM((nblk, slots, block), jnp.float32),
            pltpu.VMEM((slots, nblk, block), jnp.float32),
            pltpu.VMEM(near, jnp.float32),
            pltpu.VMEM(near, jnp.float32),
            pltpu.VMEM(mate, jnp.float32),
            pltpu.VMEM(mate, jnp.float32),
            pltpu.VMEM(tail, jnp.float32),
            pltpu.VMEM(tail, jnp.float32),
            dma((freqs,)),
            dma((freqs, PARTS)),
            dma((moves, freqs, PARTS)),
            dma((moves, freqs, PARTS)),
            dma((moves,)),
            dma((moves,)),
            dma((moves,)),
            dma((moves,)),
            dma((2,)),
            dma((2,)),
        ],
        compiler_params=pltpu.CompilerParams(
            collective_id=0, has_side_effects=True, vmem_limit_bytes=VMEM_BYTES
        ),
    )(offsets, assign, fronts, extrap)
    return images.reshape(HANDOVERS, slots // owners, points), last


def solution(mesh):
    depth = mesh.shape["depth"]

    def program(fronts, extrap, offsets, assign):
        sections = offsets.shape[0]
        placed = (
            P(None, ("groups", "depth"), None, None),
            P("depth", None, None, None, None, None),
            P(),
            P(),
        )
        return jax.shard_map(
            functools.partial(on_device, sections, depth // sections),
            mesh=mesh,
            in_specs=placed,
            out_specs=(
                P(None, ("groups", "depth"), None),
                P(None, ("groups", "depth"), None, None),
            ),
            check_vma=False,
        )(fronts, extrap, offsets, assign)

    return program
```
